32 devices in a mesh: var: 4 (over x, core), space: 8 (over z, y).
Axes of the slice: x: 2, y: 2, z: 4, core: 2. Of those that a mesh axis runs over, the one named last changes fastest.
Arguments:
- fields: bfloat16 [8, 1024, 32768], P('var', None, 'space'), may hold values from -6 to 6
- eigenfunctions: bfloat16 [8, 64, 32768], P('var', None, 'space'), may hold values from -0.03125 to 0.03125
- start: float32 [512, 128], replicated, may hold values from -6 to 6
- grid_count: int32 [8], replicated, may hold values from 16384 to 32768
Outputs:
- loadings: bfloat16 [8, 128, 32768], P('var', None, 'space')
- component_scores: float32 [1024, 128], replicated
- explained: float32 [8, 1024], P('var')
The draws below stay inside these ranges and needn't reach their ends.
Inputs may be any that keep to these rules, and one draw needn't show every extreme that they name: The grid of variable v is its points 0 to grid_count[v] - 1.
All inputs are finite; a program needn't handle non-finite values.
Results may differ from the reference program's by a relative error of at most 0.005.
Values sent between devices are 32-bit elements; how exact they have to be, the bound alone decides.
A program may use at most 64 MiB of HBM per device.

```python
import jax
import jax.numpy as jnp
from jax import lax

V = 8
M = 64
K = 128
SWEEPS = 2
NS = 1024
G = 32768
JD = 512


def with_ends(array, rng, low, high):
    shape = array.shape
    index_at = [jax.random.randint(jax.random.fold_in(rng, axis), (), 0, shape[axis]) for axis in range(len(shape))]
    array = array.at[tuple(index_at)].set(low)
    longest = shape.index(max(shape))
    index_at[longest] = (index_at[longest] + 1) % shape[longest]
    return array.at[tuple(index_at)].set(high)


def block_scale(rng, dims, pieces, low, top_value):
    level, own = 1.0, jax.random.fold_in(rng, 6)
    for dim, blocks in pieces:
        heights = jnp.exp(jax.random.uniform(jax.random.fold_in(own, dim), (blocks,), jnp.float32, low / len(pieces), top_value / len(pieces)))
        level = level * jnp.repeat(heights, dims[dim] // blocks).reshape([-1 if axis == dim else 1 for axis in range(len(dims))])
    return level


def gaussian(stream_key, dims, scale, most, split=(), kind=jnp.bfloat16):
    level = block_scale(stream_key, dims, split, -0.22, 0.18) if split else 1.0
    array = jax.random.normal(stream_key, dims, jnp.float32) * scale * level
    return jnp.minimum(jnp.maximum(array, -most), most).astype(kind)


def setup_inputs(seed: int = 0) -> dict:
    keys = jax.random.split(jax.random.key(seed), 5)
    return {
        "fields": gaussian(keys[0], (V, NS, G), 1.0, 6.0, ((0, 4), (2, 8))),
        "eigenfunctions": gaussian(keys[1], (V, M, G), G ** -0.5, 0.03125, ((0, 4), (2, 8))),
        "start": gaussian(keys[2], (JD, K), 1.0, 6.0, (), jnp.float32),
        "grid_count": with_ends(jax.random.randint(keys[3], (V,), G // 2, G + 1), jax.random.fold_in(keys[3], 1), G // 2, G).astype(jnp.int32),
    }


def orthogonalize(image):
    gram = jnp.dot(image.T.astype(jnp.float32), image.astype(jnp.float32), precision=lax.Precision.HIGHEST, preferred_element_type=jnp.float32)
    lower = jnp.linalg.cholesky(gram)
    return jax.scipy.linalg.solve_triangular(lower, image.T, lower=True).T

def reference(fields, eigenfunctions, start, grid_count):
    points = jnp.arange(G, dtype=jnp.int32)
    valid = points[None, :] < grid_count[:, None]
    masked = jnp.where(valid[:, None, :], eigenfunctions, jnp.zeros((), eigenfunctions.dtype))

    def project(pair):
        return jnp.dot(pair[0].astype(jnp.float32), pair[1].T.astype(jnp.float32), preferred_element_type=jnp.float32)
    scores = lax.map(project, (fields, masked))
    joint = jnp.transpose(scores, (1, 0, 2)).reshape(NS, V * M)
    centred = joint - jnp.mean(joint, axis=0, keepdims=True)
    cov = jnp.dot(centred.T.astype(jnp.float32), centred.astype(jnp.float32), precision=lax.Precision.HIGHEST, preferred_element_type=jnp.float32) / (NS - 1)
    basis = start
    for sweep in range(SWEEPS):
        image = jnp.dot(cov.astype(jnp.float32), basis.astype(jnp.float32), precision=lax.Precision.HIGHEST, preferred_element_type=jnp.float32)
        basis = orthogonalize(image)
    component_scores = jnp.dot(centred.astype(jnp.float32), basis.astype(jnp.float32), precision=lax.Precision.HIGHEST, preferred_element_type=jnp.float32)
    basis_low = basis.astype(jnp.bfloat16).reshape(V, M, K)
    scores_low = component_scores.astype(jnp.bfloat16)

    def rebuild(trio):
        values, funcs, coeffs = trio
        loading = jnp.dot(coeffs.T.astype(jnp.float32), funcs.astype(jnp.float32), preferred_element_type=jnp.float32).astype(jnp.bfloat16)
        rebuilt = jnp.dot(scores_low.astype(jnp.float32), loading.astype(jnp.float32), preferred_element_type=jnp.float32)
        wide = values.astype(jnp.float32)
        deviation = wide - jnp.mean(wide, axis=0, keepdims=True)
        gain = jnp.sum(2.0 * deviation * rebuilt - rebuilt * rebuilt, axis=1) / M
        return (loading, gain)
    loadings, explained = lax.map(rebuild, (fields, masked, basis_low))
    return (loadings, component_scores, explained)
```

```python
import functools

import jax
import jax.numpy as jnp
from jax import lax
from jax.experimental import pallas as pl
from jax.experimental.pallas import tpu as pltpu
from jax.sharding import PartitionSpec as P

M = 64
SWEEPS = 2
MESH = pl.DeviceIdType.MESH
F32 = jnp.float32
BF16 = jnp.bfloat16
HIGHEST = lax.Precision.HIGHEST


def dot(left, right, dims, precision=None):
    return lax.dot_general(left, right, (dims, ((), ())), precision=precision, preferred_element_type=F32)


NN = ((1,), (0,))
NT = ((1,), (1,))
TN = ((0,), (0,))


def split(x):
    high = x.astype(BF16)
    return high, (x - high.astype(F32)).astype(BF16)


def dot3(left, right, dims):
    (lh, ll), (rh, rl) = left, right
    return dot(lh, rh, dims) + (dot(lh, rl, dims) + dot(ll, rh, dims))


def remote(src, dst, send, recv, target):
    return pltpu.make_async_remote_copy(
        src_ref=src, dst_ref=dst, send_sem=send, recv_sem=recv, device_id=target, device_id_type=MESH
    )


def masked_block(count, eigen, first):
    points = first + lax.broadcasted_iota(jnp.int32, (1, eigen.shape[1]), 1)
    return eigen * jnp.where(points < count, 1.0, 0.0).astype(eigen.dtype)


def gather_kernel(
    n, pieces, counts_hbm, fields, eigen_hbm, centred_ref, gram_ref, masked_ref,
    counts, eigen, fbuf, weights, part, rbuf, cross, jbuf, gpart, grbuf, gred, gfull,
    csem, esem, fsem, rsend, rrecv, xsend, xrecv, asend, arecv, psend, precv, gsend, grecv, hsend, hrecv,
):
    var, me = lax.axis_index("var"), lax.axis_index("space")
    local_vars, samples, local_points = fields.shape
    rows = samples // (4 * pieces)
    width = local_vars * M
    groups = n // 4
    side, core = var // 2, lax.rem(var, 2)
    group, quad = me // 4, lax.rem(me, 4)
    depth, lane_y = quad // 2, lax.rem(quad, 2)
    far, mate = 1 - side, 1 - core

    def owner(dz, dy):
        return 2 * (depth + dz - 2 * depth * dz) + lane_y + dy - 2 * lane_y * dy

    def fetch(i):
        first = (4 * (i // 2) + 2 * (owner(1 - lax.rem(i, 2), 0) // 2)) * rows
        block = pl.ds(pl.multiple_of(first, 2 * rows), 2 * rows)
        return pltpu.make_async_copy(fields.at[:, block, :], fbuf.at[i], fsem.at[i])

    eigen_copy = pltpu.make_async_copy(eigen_hbm, eigen, esem)
    counts_copy = pltpu.make_async_copy(counts_hbm, counts, csem)
    counts_copy.start()
    eigen_copy.start()
    lax.fori_loop(0, 2 * pieces, lambda i, carry: (fetch(i).start(), carry)[1], 0)

    xside, yside, zside = (2 * far + mate, me), (2 * side + mate, 4 * group + owner(0, 1)), (2 * side + mate, 4 * group + owner(1, 0))
    corner, partner = (2 * far + mate, 4 * group + owner(1, 1)), (2 * side + mate, me)
    barrier = pltpu.get_barrier_semaphore()
    for d in range(1, n):
        pl.semaphore_signal(barrier, inc=1, device_id=(var, lax.rem(me + d, n)), device_id_type=MESH)
    for target in (xside, yside, zside, corner, partner):
        pl.semaphore_signal(barrier, inc=1, device_id=target, device_id_type=MESH)

    counts_copy.wait()
    eigen_copy.wait()
    for v in range(local_vars):
        masked = masked_block(counts[var * local_vars + v], eigen[v], me * local_points)
        masked_ref[v] = masked
        weights[:, v * M:(v + 1) * M] = masked.T

    pl.semaphore_wait(barrier, n - 1 + 5)

    def send_part(p, k):
        j = 3 * p + k
        source = part.at[2 * p + k // 2, 1 - lane_y if k % 2 == 0 else lane_y]
        target = (var, 4 * group + owner(1 - k // 2, 1 - k % 2))
        return remote(source, rbuf.at[j], rsend.at[j], rrecv.at[j], target)

    column = lax.broadcasted_iota(jnp.int32, (2 * rows, width), 1) // M

    def project(i):
        fetch(i).wait()
        scores = dot(fbuf[i, 0], weights[...], NN)
        for v in range(1, local_vars):
            scores = jnp.where(column == v, dot(fbuf[i, v], weights[...], NN), scores)
        part[i, 0] = scores[0:rows]
        part[i, 1] = scores[rows:2 * rows]

    def step(p, carry):
        @pl.when(p > 0)
        def _():
            send_part(p - 1, 2).start()

        project(2 * p)
        send_part(p, 0).start()
        send_part(p, 1).start()
        project(2 * p + 1)
        return carry

    def block(p, origin, o):
        return jbuf.at[origin, pl.ds(pl.multiple_of((4 * p + o) * rows, rows), rows)]

    own = [block(p, var, quad) for p in range(pieces)]

    def send_cross(p, d):
        j = p * (groups - 1) + d - 1
        target = (var, 4 * lax.rem(group + d, groups) + quad)
        return remote(cross.at[p, group], cross.at[p, group], xsend.at[j], xrecv.at[j], target)

    def half_sum(p):
        total = part[2 * p + 1, lane_y]
        for k in range(3):
            send_part(p, k).wait_recv()
            total = total + rbuf[3 * p + k]
        cross[p, group] = total
        for d in range(1, groups):
            send_cross(p, d).start()

    def relation(p, kind):
        return {
            "x": lambda: block(p, 2 * far + mate, quad),
            "y": lambda: block(p, 2 * side + mate, owner(0, 1)),
            "z": lambda: block(p, 2 * side + mate, owner(1, 0)),
            "xy": lambda: block(p, 2 * far + core, owner(0, 1)),
            "xz": lambda: block(p, 2 * far + core, owner(1, 0)),
            "yz": lambda: block(p, 2 * side + core, owner(1, 1)),
            "xyz": lambda: block(p, 2 * far + mate, owner(1, 1)),
        }[kind]()

    kinds = ("x", "y", "z", "xy", "xz", "yz", "xyz")

    def route(p, kind):
        last = (("xyz", "yz", xside), ("xyz", "xz", yside), ("xyz", "xy", zside))[p % 3]
        if p == pieces - 1:
            last = ("xyz", "", corner)
        return {
            "x": ("", xside), "y": ("", yside), "z": ("", zside),
            "xz": ("x", zside), "xy": ("y", xside), "yz": ("z", yside), "xyz": last[1:],
        }[kind]

    def send_on(p, kind):
        source, target = route(p, kind)
        piece = own[p] if source == "" else relation(p, source)
        j = p * 7 + kinds.index(kind)
        return remote(piece, piece, asend.at[j], arecv.at[j], target)

    def share(p, kind):
        piece = own[p] if kind == "" else relation(p, kind)
        j = p * 8 + (7 if kind == "" else kinds.index(kind))
        return remote(piece, piece, psend.at[j], precv.at[j], partner)

    def arrived(p, kind):
        send_on(p, kind).wait_recv()
        for other in kinds:
            if route(p, other)[0] == kind:
                send_on(p, other).start()
        share(p, kind).start()

    def full_sum(p):
        for d in range(1, groups):
            send_cross(p, d).wait_recv()
        total = cross[p, 0]
        for g in range(1, groups):
            total = total + cross[p, g]
        own[p][...] = total
        for kind in kinds:
            if route(p, kind)[0] == "":
                send_on(p, kind).start()
        share(p, "").start()

    def first_hop(p):
        for kind in ("x", "y", "z"):
            arrived(p, kind)

    def second_hop(p):
        for kind in ("xy", "xz", "yz"):
            arrived(p, kind)

    def third_hop(p):
        arrived(p, "xyz")

    grows = M // n

    def send_gram(d):
        target = lax.rem(me + d, n)
        return remote(gpart.at[target], grbuf.at[d - 1], gsend.at[d - 1], grecv.at[d - 1], (var, target))

    def send_gfull(d):
        return remote(gred, gfull.at[me], hsend.at[d - 1], hrecv.at[d - 1], (var, lax.rem(me + d, n)))

    def gram_parts():
        grams = [dot(masked_ref[v], masked_ref[v], NT) for v in range(local_vars)]
        gram = jnp.concatenate(grams, axis=1)
        gpart[...] = jnp.zeros_like(gpart)
        for s in range(n):
            gpart[s, 0:grows, :] = gram[s * grows:(s + 1) * grows, :]
        for d in range(1, n):
            send_gram(d).start()

    def gram_sum():
        gtotal = gpart[me]
        for d in range(1, n):
            send_gram(d).wait()
            gtotal = gtotal + grbuf[d - 1]
        gred[...] = gtotal
        gfull[me] = gtotal
        for d in range(1, n):
            send_gfull(d).start()

    stages = (half_sum, full_sum, first_hop, second_hop, third_hop)
    early = max(pieces - 1, 1)
    lax.fori_loop(0, early, step, 0)
    half_sum(0)
    lax.fori_loop(early, pieces, step, 0)
    send_part(pieces - 1, 2).start()
    gram_parts()
    slots = sorted((1.5 * p + (0, 2.2, 3.8, 5.4, 7.0)[s], s, p) for s in range(5) for p in range(pieces))
    for at, s, p in slots[1:]:
        if (s, p) == (2, pieces - 1):
            gram_sum()
        stages[s](p)

    for d in range(1, n):
        send_gfull(d).wait()
    for p in range(pieces):
        for k in range(3):
            send_part(p, k).wait_send()
        for d in range(1, groups):
            send_cross(p, d).wait_send()
        for kind in kinds:
            send_on(p, kind).wait_send()
        for kind in kinds + ("",):
            share(p, kind).wait()

    for v in range(2 * (jbuf.shape[0] // 2)):
        mean = jnp.sum(jbuf[v], axis=0, keepdims=True) / samples
        centred_ref[:, v * width:(v + 1) * width] = jbuf[v] - mean
    for s in range(n):
        gram_ref[s * grows:(s + 1) * grows, :] = gfull[s, 0:grows, :]


def gather_scores(n, nv, counts, fields, eigen):
    local_vars, samples, points = fields.shape
    pieces = 4
    if nv != 4 or n % 4 or samples % (4 * pieces):
        raise ValueError("unsupported mesh")
    rows = samples // (4 * pieces)
    width = local_vars * M
    groups = n // 4
    dma = pltpu.SemaphoreType.DMA
    pairs = [3 * pieces, max(1, pieces * (groups - 1)), 7 * pieces, 8 * pieces, n - 1, n - 1]
    return pl.pallas_call(
        functools.partial(gather_kernel, n, pieces),
        out_shape=(
            jax.ShapeDtypeStruct((samples, nv * width), F32),
            jax.ShapeDtypeStruct((M, width), F32),
            jax.ShapeDtypeStruct((local_vars, M, points), BF16),
        ),
        in_specs=[pl.BlockSpec(memory_space=pltpu.HBM)] * 3,
        out_specs=(pl.BlockSpec(memory_space=pltpu.VMEM),) * 3,
        scratch_shapes=[
            pltpu.SMEM(counts.shape, jnp.int32),
            pltpu.VMEM((local_vars, M, points), BF16),
            pltpu.VMEM((2 * pieces, local_vars, 2 * rows, points), BF16),
            pltpu.VMEM((points, width), BF16),
            pltpu.VMEM((2 * pieces, 2, rows, width), F32),
            pltpu.VMEM((3 * pieces, rows, width), F32),
            pltpu.VMEM((pieces, groups, rows, width), F32),
            pltpu.VMEM((nv, samples, width), F32),
            pltpu.VMEM((n, 8, width), F32),
            pltpu.VMEM((n - 1, 8, width), F32),
            pltpu.VMEM((8, width), F32),
            pltpu.VMEM((n, 8, width), F32),
            dma(()),
            dma(()),
            dma((2 * pieces,)),
            *[dma((count,)) for count in pairs for _ in range(2)],
        ],
        compiler_params=pltpu.CompilerParams(
            collective_id=0, has_side_effects=True, vmem_limit_bytes=48 * 1024 * 1024
        ),
        name="gather_scores",
    )(*(pltpu.with_memory_space_constraint(x, pltpu.HBM) for x in (counts, fields, eigen)))


def inverse_factor(gram):
    size = gram.shape[0]
    tiles = size // 8
    rows = [gram[8 * i:8 * i + 8, :] for i in range(tiles)]
    lane = lax.broadcasted_iota(jnp.int32, (8, size), 1)
    sublane = lax.broadcasted_iota(jnp.int32, (8, size), 0)

    def columns(tile, b):
        return [jnp.broadcast_to(tile[:, 8 * b + j:8 * b + j + 1], (8, size)) for j in range(8)]

    def spread(tile, j):
        return jnp.broadcast_to(tile[j:j + 1, :], (8, size))

    done = []
    block = columns(rows[0], 0)
    for b in range(tiles):
        inside = (lane >= 8 * b) & (lane < 8 * b + 8)
        work = jnp.where(inside, jnp.where(lane - 8 * b == sublane, 1.0, 0.0), rows[b])
        inverse, cross, lower = [], {}, []
        pivot = None
        for j in range(8):
            diagonal = spread(block[j], j)
            pivot = diagonal if j == 0 else jnp.where(sublane == j, diagonal, pivot)
            inverse.append(1.0 / diagonal)
            for q in range(j + 1, 8):
                cross[j, q] = spread(block[j], q)
            if j == 7:
                break
            block[j + 1] = block[j + 1] - (block[j] * cross[j, j + 1]) * inverse[j]
            factor = block[j] * inverse[j]
            lower.append(factor)
            for q in range(j + 2, 8):
                block[q] = block[q] - factor * cross[j, q]
            work = work - jnp.where(sublane > j, factor, 0.0) * spread(work, j)
        done.append(jnp.where(lane < 8 * b + 8, work, 0.0) * lax.rsqrt(pivot))
        if b + 1 == tiles:
            break
        line = [spread(work, j) for j in range(8)]
        for i in range(b + 1, min(b + 3, tiles)):
            value, factors = columns(rows[i], b), []
            for j in range(8):
                factors.append(value[j] * inverse[j])
                for q in range(j + 1, 8):
                    value[q] = value[q] - factors[j] * cross[j, q]
            if i == b + 1:
                block = columns(rows[i], i)
                for q in range(8):
                    for j in range(8):
                        block[q] = block[q] - factors[j] * spread(value[j], q)
            new = jnp.where(inside, 0.0, rows[i])
            for j in range(8):
                new = new - factors[j] * line[j]
            rows[i] = new
        if b + 3 >= tiles:
            continue
        solved = [None] * 8
        for j in reversed(range(8)):
            value = line[j] * inverse[j]
            for q in range(j + 1, 8):
                value = value - spread(lower[j], q) * solved[q]
            solved[j] = value
        for i in range(b + 3, tiles):
            new = jnp.where(inside, 0.0, rows[i])
            entry = columns(rows[i], b)
            for j in range(8):
                new = new - entry[j] * solved[j]
            rows[i] = new
    return done


def basis_kernel(
    centred_ref, gram_ref, start_ref, masked_ref, loadings_ref, scores_ref, explained_ref,
    high_ref, low_ref, cov_high, cov_low, basis_ref, inverse_ref,
):
    var = lax.axis_index("var")
    samples = centred_ref.shape[0]
    local_vars = masked_ref.shape[0]
    width = local_vars * M
    high, low = split(centred_ref[...])
    high_ref[...] = high
    low_ref[...] = low
    cov = dot3((high, low), (high, low), TN) / (samples - 1)
    cov_high[...], cov_low[...] = split(cov)
    basis_ref[...] = start_ref[...]

    def sweep(_, carry):
        image = dot3((cov_high[...], cov_low[...]), split(basis_ref[...]), NN)
        gram = dot(image, image, TN, HIGHEST)
        for i, tile in enumerate(inverse_factor(gram)):
            inverse_ref[8 * i:8 * i + 8, :] = tile
        basis_ref[...] = dot(image, inverse_ref[...], NT, HIGHEST)
        return carry

    lax.fori_loop(0, SWEEPS, sweep, 0)

    scores = dot3((high_ref[...], low_ref[...]), split(basis_ref[...]), NN)
    scores_ref[...] = scores
    scores_low = scores.astype(BF16)
    own = pl.ds(pl.multiple_of(var * width, width), width)
    basis_low = basis_ref[own, :].astype(BF16)
    own_high, own_low = high_ref[:, own], low_ref[:, own]
    ones = jnp.ones((8, basis_low.shape[1]), F32)
    scores_wide = scores_low.astype(F32)
    for v in range(local_vars):
        mine = basis_low[v * M:(v + 1) * M, :]
        loadings_ref[v] = dot(mine, masked_ref[v], TN).astype(BF16)
        left, right = own_high[:, v * M:(v + 1) * M], own_low[:, v * M:(v + 1) * M]
        cross = dot(left, mine, NN) + dot(right, mine, NN)
        wide = mine.astype(F32)
        inner = dot(gram_ref[:, v * M:(v + 1) * M], wide, NN, HIGHEST)
        square = split(dot(wide, inner, TN, HIGHEST))
        quad = dot(scores_low, square[0], NN) + dot(scores_low, square[1], NN)
        gain = scores_wide * (2.0 * cross - quad)
        summed = dot(ones, gain, NT, HIGHEST) / M
        explained_ref[v:v + 1, :] = summed[0:1, :]


def finish(centred, gram, start, masked):
    local_vars, _, points = masked.shape
    samples, joint = centred.shape
    k = start.shape[1]
    return pl.pallas_call(
        basis_kernel,
        out_shape=(
            jax.ShapeDtypeStruct((local_vars, k, points), BF16),
            jax.ShapeDtypeStruct((samples, k), F32),
            jax.ShapeDtypeStruct((local_vars, samples), F32),
        ),
        in_specs=[pl.BlockSpec(memory_space=pltpu.VMEM)] * 4,
        out_specs=(pl.BlockSpec(memory_space=pltpu.VMEM),) * 3,
        scratch_shapes=[
            pltpu.VMEM((samples, joint), BF16),
            pltpu.VMEM((samples, joint), BF16),
            pltpu.VMEM((joint, joint), BF16),
            pltpu.VMEM((joint, joint), BF16),
            pltpu.VMEM((joint, k), F32),
            pltpu.VMEM((k, k), F32),
        ],
        compiler_params=pltpu.CompilerParams(vmem_limit_bytes=48 * 1024 * 1024),
        name="finish",
    )(centred, gram, start, masked)


def shards(n, nv, fields, eigenfunctions, start, grid_count):
    centred, gram, masked = gather_scores(n, nv, grid_count, fields, eigenfunctions)
    return finish(centred, gram, start, masked)


def solution(mesh):
    return jax.shard_map(
        functools.partial(shards, mesh.shape["space"], mesh.shape["var"]),
        mesh=mesh,
        in_specs=(P("var", None, "space"), P("var", None, "space"), P(), P()),
        out_specs=(P("var", None, "space"), P(), P("var", None)),
        check_vma=False,
    )
```

```python
import functools

import jax
import jax.numpy as jnp
from jax import lax
from jax.experimental import pallas as pl
from jax.experimental.pallas import tpu as pltpu
from jax.sharding import PartitionSpec as P

M = 64
SWEEPS = 2
MESH = pl.DeviceIdType.MESH
F32 = jnp.float32
BF16 = jnp.bfloat16
HIGHEST = lax.Precision.HIGHEST


def dot(left, right, dims, precision=None):
    return lax.dot_general(left, right, (dims, ((), ())), precision=precision, preferred_element_type=F32)


NN = ((1,), (0,))
NT = ((1,), (1,))
TN = ((0,), (0,))


def split(x):
    high = x.astype(BF16)
    return high, (x - high.astype(F32)).astype(BF16)


def dot3(left, right, dims):
    (lh, ll), (rh, rl) = left, right
    return dot(lh, rh, dims) + (dot(lh, rl, dims) + dot(ll, rh, dims))


def remote(src, dst, send, recv, target):
    return pltpu.make_async_remote_copy(
        src_ref=src, dst_ref=dst, send_sem=send, recv_sem=recv, device_id=target, device_id_type=MESH
    )


def masked_block(count, eigen, first):
    points = first + lax.broadcasted_iota(jnp.int32, (1, eigen.shape[1]), 1)
    return eigen * jnp.where(points < count, 1.0, 0.0).astype(eigen.dtype)


SHARES = (4, 4, 4, 2, 2)
AHEAD = 3


def layout(samples):
    unit = samples // (4 * sum(SHARES))
    rows = [unit * share for share in SHARES]
    return rows, [sum(rows[:p]) for p in range(len(rows))]


def gather_kernel(
    n, counts_hbm, fields, eigen_hbm, high_ref, low_ref, cov_high, cov_low, shift_ref, gram_ref, masked_ref,
    counts, eigen, moment, fbuf, weights, part, rbuf, cross, jbuf, gpart, grbuf, gred, gfull,
    csem, esem, fsem, rsend, rrecv, xsend, xrecv, asend, arecv, psend, precv, gsend, grecv, hsend, hrecv,
):
    var, me = lax.axis_index("var"), lax.axis_index("space")
    local_vars, samples, local_points = fields.shape
    rows, start = layout(samples)
    pieces = len(rows)
    chunk = 2 * rows[0]
    full = sum(size == rows[0] for size in rows)
    width = local_vars * M
    groups = n // 4
    side, core = var // 2, lax.rem(var, 2)
    group, quad = me // 4, lax.rem(me, 4)
    depth, lane_y = quad // 2, lax.rem(quad, 2)
    far, mate = 1 - side, 1 - core

    def owner(dz, dy):
        return 2 * (depth + dz - 2 * depth * dz) + lane_y + dy - 2 * lane_y * dy

    def fetch(i):
        swapped = 2 * (i // 2) + lax.rem(depth + 1 + i, 2)
        first = chunk * jnp.where(i < 2 * full, swapped, i)
        block = pl.ds(pl.multiple_of(first, chunk), chunk)
        return pltpu.make_async_copy(fields.at[:, block, :], fbuf.at[i], fsem.at[i])

    eigen_copy = pltpu.make_async_copy(eigen_hbm, eigen, esem)
    counts_copy = pltpu.make_async_copy(counts_hbm, counts, csem)
    counts_copy.start()
    eigen_copy.start()
    for i in range(min(2, samples // chunk)):
        fetch(i).start()

    xside, yside, zside = (2 * far + mate, me), (2 * side + mate, 4 * group + owner(0, 1)), (2 * side + mate, 4 * group + owner(1, 0))
    corner, partner = (2 * far + mate, 4 * group + owner(1, 1)), (2 * side + mate, me)
    barrier = pltpu.get_barrier_semaphore()
    for d in range(1, n):
        pl.semaphore_signal(barrier, inc=1, device_id=(var, lax.rem(me + d, n)), device_id_type=MESH)
    for target in (xside, yside, zside, corner, partner):
        pl.semaphore_signal(barrier, inc=1, device_id=target, device_id_type=MESH)

    counts_copy.wait()
    eigen_copy.wait()
    for i in range(2, min(AHEAD, samples // chunk)):
        fetch(i).start()
    for v in range(local_vars):
        masked = masked_block(counts[var * local_vars + v], eigen[v], me * local_points)
        masked_ref[v] = masked
        weights[v * M:(v + 1) * M, :] = masked

    pl.semaphore_wait(barrier, n - 1 + 5)

    def span(p, o):
        return pl.ds(pl.multiple_of(4 * start[p] + o * rows[p], 8), rows[p])

    def send_part(p, k):
        o = owner(1 - k // 2, 1 - k % 2)
        if isinstance(p, int):
            source = part.at[span(p, o)]
            slot = rbuf.at[pl.ds(3 * start[p] + k * rows[p], rows[p])]
        else:
            source = part.at[pl.ds(pl.multiple_of((4 * p + o) * rows[0], 8), rows[0])]
            slot = rbuf.at[pl.ds(pl.multiple_of((3 * p + k) * rows[0], 8), rows[0])]
        j = 3 * p + k
        return remote(source, slot, rsend.at[j], rrecv.at[j], (var, 4 * group + o))

    column = lax.broadcasted_iota(jnp.int32, (chunk, width), 1) // M

    def project(i, first):
        later = i + AHEAD
        if not isinstance(i, int):
            pl.when(later < samples // chunk)(lambda: fetch(later).start())
        elif later < samples // chunk:
            fetch(later).start()
        fetch(i).wait()
        scores = dot(fbuf[i, 0], weights[...], NT)
        for v in range(1, local_vars):
            scores = jnp.where(column == v, dot(fbuf[i, v], weights[...], NT), scores)
        part[pl.ds(pl.multiple_of(first, chunk), chunk), :] = scores

    def step(p, carry):
        @pl.when(p > 0)
        def _():
            send_part(p - 1, 2).start()

        project(2 * p, chunk * (2 * p + 1 - depth))
        send_part(p, 0).start()
        send_part(p, 1).start()
        project(2 * p + 1, chunk * (2 * p + depth))
        return carry

    def block(p, origin, o):
        return jbuf.at[origin, span(p, o)]

    own = [block(p, var, quad) for p in range(pieces)]

    def held(p):
        return pl.ds(start[p], rows[p])

    def send_cross(p, d):
        j = p * (groups - 1) + d - 1
        target = (var, 4 * lax.rem(group + d, groups) + quad)
        return remote(cross.at[group, held(p)], cross.at[group, held(p)], xsend.at[j], xrecv.at[j], target)

    def half_sum(p):
        total = part[span(p, quad), :]
        for k in range(3):
            send_part(p, k).wait_recv()
            first = 3 * start[p] + k * rows[p]
            total = total + rbuf[first:first + rows[p], :]
        cross[group, held(p)] = total
        for d in range(1, groups):
            send_cross(p, d).start()

    def relation(p, kind):
        return {
            "x": lambda: block(p, 2 * far + mate, quad),
            "y": lambda: block(p, 2 * side + mate, owner(0, 1)),
            "z": lambda: block(p, 2 * side + mate, owner(1, 0)),
            "xy": lambda: block(p, 2 * far + core, owner(0, 1)),
            "xz": lambda: block(p, 2 * far + core, owner(1, 0)),
            "yz": lambda: block(p, 2 * side + core, owner(1, 1)),
            "xyz": lambda: block(p, 2 * far + mate, owner(1, 1)),
        }[kind]()

    kinds = ("x", "y", "z", "xy", "xz", "yz", "xyz")

    def route(p, kind):
        last = ("yz", xside) if p == 0 else ("", corner)
        return {
            "x": ("", xside), "y": ("", yside), "z": ("", zside),
            "xz": ("x", zside), "xy": ("y", xside), "yz": ("z", yside), "xyz": last,
        }[kind]

    def send_on(p, kind):
        source, target = route(p, kind)
        piece = own[p] if source == "" else relation(p, source)
        j = p * 7 + kinds.index(kind)
        return remote(piece, piece, asend.at[j], arecv.at[j], target)

    def share(p, kind):
        piece = own[p] if kind == "" else relation(p, kind)
        j = p * 8 + (7 if kind == "" else kinds.index(kind))
        return remote(piece, piece, psend.at[j], precv.at[j], partner)

    def arrived(p, kind):
        send_on(p, kind).wait_recv()
        for other in kinds:
            if route(p, other)[0] == kind:
                send_on(p, other).start()
        share(p, kind).start()

    def full_sum(p):
        for d in range(1, groups):
            send_cross(p, d).wait_recv()
        total = cross[0, held(p)]
        for g in range(1, groups):
            total = total + cross[g, held(p)]
        own[p][...] = total
        for kind in kinds:
            if route(p, kind)[0] == "":
                send_on(p, kind).start()
        share(p, "").start()

    def first_hop(p):
        for kind in ("x", "y", "z"):
            arrived(p, kind)

    def second_hop(p):
        for kind in ("xy", "xz", "yz"):
            arrived(p, kind)

    def third_hop(p):
        arrived(p, "xyz")

    def moments(first, last, initial):
        for p in range(first, last + 1):
            for kind in kinds + ("",):
                share(p, kind).wait_recv()
        place = slice(4 * start[first], 4 * (start[last] + rows[last]))
        block = jnp.concatenate([jbuf[v, place, :] for v in range(jbuf.shape[0])], axis=1)
        if initial:
            shift_ref[0:1, :] = jnp.sum(block, axis=0, keepdims=True) / block.shape[0]
        block = block - shift_ref[0:1, :]
        total = jnp.sum(block, axis=0, keepdims=True)
        high, low = split(block)
        high_ref[place, :] = high
        low_ref[place, :] = low
        square = dot3((high, low), (high, low), TN)
        shift_ref[1:2, :] = total if initial else shift_ref[1:2, :] + total
        moment[...] = square if initial else moment[...] + square

    grows = M // n

    def send_gram(d):
        target = lax.rem(me + d, n)
        return remote(gpart.at[target], grbuf.at[d - 1], gsend.at[d - 1], grecv.at[d - 1], (var, target))

    def send_gfull(d):
        return remote(gred, gfull.at[me], hsend.at[d - 1], hrecv.at[d - 1], (var, lax.rem(me + d, n)))

    def gram_parts():
        grams = [dot(masked_ref[v], masked_ref[v], NT) for v in range(local_vars)]
        gram = jnp.concatenate(grams, axis=1)
        gpart[...] = jnp.zeros_like(gpart)
        for s in range(n):
            gpart[s, 0:grows, :] = gram[s * grows:(s + 1) * grows, :]
        for d in range(1, n):
            send_gram(d).start()

    def gram_sum():
        gtotal = gpart[me]
        for d in range(1, n):
            send_gram(d).wait()
            gtotal = gtotal + grbuf[d - 1]
        gred[...] = gtotal
        gfull[me] = gtotal
        for d in range(1, n):
            send_gfull(d).start()

    lax.fori_loop(0, full, step, 0)
    send_part(full - 1, 2).start()
    half_sum(0)
    for p in range(full, pieces):
        project(full + p, chunk * (full + p))
        for k in range(3):
            send_part(p, k).start()
    gram_parts()
    order = (
        (0, 1), (0, 2), (0, 3), (1, 0), (0, 4), (1, 1), (2, 0), (1, 2), (1, 3), (1, 4), (5, 0), (2, 1), (3, 0),
        (2, 2), (2, 3), (2, 4), (3, 1), (4, 1), (4, 0), (3, 2), (4, 2), (3, 3), (4, 3), (3, 4), (4, 4),
    )
    for stage, p in order:
        if stage == 5:
            gram_sum()
        else:
            (half_sum, full_sum, first_hop, second_hop, third_hop)[stage](p)
    moments(1, 1, True)
    moments(0, 0, False)
    moments(2, 2, False)
    moments(3, 4, False)

    for d in range(1, n):
        send_gfull(d).wait()
    for p in range(pieces):
        for k in range(3):
            send_part(p, k).wait_send()
        for d in range(1, groups):
            send_cross(p, d).wait_send()
        for kind in kinds:
            send_on(p, kind).wait_send()
        for kind in kinds + ("",):
            share(p, kind).wait_send()

    offset = shift_ref[1:2, :] / samples
    shift_ref[0:1, :] = offset
    tall = jnp.where(lax.broadcasted_iota(jnp.int32, (16, offset.shape[1]), 0) == 0, offset, 0.0)
    outer = split(tall)
    cov = (moment[...] - samples * dot3(outer, outer, TN)) / (samples - 1)
    cov_high[...], cov_low[...] = split(cov)
    for s in range(n):
        gram_ref[s * grows:(s + 1) * grows, :] = gfull[s, 0:grows, :]


def gather_scores(n, nv, counts, fields, eigen):
    local_vars, samples, points = fields.shape
    rows, _ = layout(samples)
    pieces = len(rows)
    if nv != 4 or n % 4 or samples % (64 * sum(SHARES)):
        raise ValueError("unsupported mesh")
    chunk = 2 * rows[0]
    quarter = samples // 4
    width = local_vars * M
    groups = n // 4
    dma = pltpu.SemaphoreType.DMA
    pairs = [3 * pieces, max(1, pieces * (groups - 1)), 7 * pieces, 8 * pieces, n - 1, n - 1]
    return pl.pallas_call(
        functools.partial(gather_kernel, n),
        out_shape=(
            jax.ShapeDtypeStruct((samples, nv * width), BF16),
            jax.ShapeDtypeStruct((samples, nv * width), BF16),
            jax.ShapeDtypeStruct((nv * width, nv * width), BF16),
            jax.ShapeDtypeStruct((nv * width, nv * width), BF16),
            jax.ShapeDtypeStruct((8, nv * width), F32),
            jax.ShapeDtypeStruct((M, width), F32),
            jax.ShapeDtypeStruct((local_vars, M, points), BF16),
        ),
        in_specs=[pl.BlockSpec(memory_space=pltpu.HBM)] * 3,
        out_specs=(pl.BlockSpec(memory_space=pltpu.VMEM),) * 7,
        scratch_shapes=[
            pltpu.SMEM(counts.shape, jnp.int32),
            pltpu.VMEM((local_vars, M, points), BF16),
            pltpu.VMEM((nv * width, nv * width), F32),
            pltpu.VMEM((samples // chunk, local_vars, chunk, points), BF16),
            pltpu.VMEM((width, points), BF16),
            pltpu.VMEM((samples, width), F32),
            pltpu.VMEM((3 * quarter, width), F32),
            pltpu.VMEM((groups, quarter, width), F32),
            pltpu.VMEM((nv, samples, width), F32),
            pltpu.VMEM((n, 8, width), F32),
            pltpu.VMEM((n - 1, 8, width), F32),
            pltpu.VMEM((8, width), F32),
            pltpu.VMEM((n, 8, width), F32),
            dma(()),
            dma(()),
            dma((samples // chunk,)),
            *[dma((count,)) for count in pairs for _ in range(2)],
        ],
        compiler_params=pltpu.CompilerParams(
            collective_id=0, has_side_effects=True, vmem_limit_bytes=48 * 1024 * 1024
        ),
        name="gather_scores",
    )(*(pltpu.with_memory_space_constraint(x, pltpu.HBM) for x in (counts, fields, eigen)))


def inverse_factor(gram):
    size = gram.shape[0]
    tiles = size // 8
    rows = [gram[8 * i:8 * i + 8, :] for i in range(tiles)]
    lane = lax.broadcasted_iota(jnp.int32, (8, size), 1)
    sublane = lax.broadcasted_iota(jnp.int32, (8, size), 0)

    def columns(tile, b):
        return [jnp.broadcast_to(tile[:, 8 * b + j:8 * b + j + 1], (8, size)) for j in range(8)]

    def spread(tile, j):
        return jnp.broadcast_to(tile[j:j + 1, :], (8, size))

    done = []
    block = columns(rows[0], 0)
    for b in range(tiles):
        inside = (lane >= 8 * b) & (lane < 8 * b + 8)
        work = jnp.where(inside, jnp.where(lane - 8 * b == sublane, 1.0, 0.0), rows[b])
        inverse, cross, lower = [], {}, []
        pivot = None
        for j in range(8):
            diagonal = spread(block[j], j)
            pivot = diagonal if j == 0 else jnp.where(sublane == j, diagonal, pivot)
            inverse.append(1.0 / diagonal)
            for q in range(j + 1, 8):
                cross[j, q] = spread(block[j], q)
            if j == 7:
                break
            block[j + 1] = block[j + 1] - (block[j] * cross[j, j + 1]) * inverse[j]
            factor = block[j] * inverse[j]
            lower.append(factor)
            for q in range(j + 2, 8):
                block[q] = block[q] - factor * cross[j, q]
            work = work - jnp.where(sublane > j, factor, 0.0) * spread(work, j)
        done.append(jnp.where(lane < 8 * b + 8, work, 0.0) * lax.rsqrt(pivot))
        if b + 1 == tiles:
            break
        line = [spread(work, j) for j in range(8)]
        for i in range(b + 1, min(b + 3, tiles)):
            value, factors = columns(rows[i], b), []
            for j in range(8):
                factors.append(value[j] * inverse[j])
                for q in range(j + 1, 8):
                    value[q] = value[q] - factors[j] * cross[j, q]
            if i == b + 1:
                block = columns(rows[i], i)
                for q in range(8):
                    for j in range(8):
                        block[q] = block[q] - factors[j] * spread(value[j], q)
            new = jnp.where(inside, 0.0, rows[i])
            for j in range(8):
                new = new - factors[j] * line[j]
            rows[i] = new
        if b + 3 >= tiles:
            continue
        solved = [None] * 8
        for j in reversed(range(8)):
            value = line[j] * inverse[j]
            for q in range(j + 1, 8):
                value = value - spread(lower[j], q) * solved[q]
            solved[j] = value
        for i in range(b + 3, tiles):
            new = jnp.where(inside, 0.0, rows[i])
            entry = columns(rows[i], b)
            for j in range(8):
                new = new - entry[j] * solved[j]
            rows[i] = new
    return done


def packed(left, right):
    (lh, ll), (rh, rl) = left, right
    k = rh.shape[1]
    both = dot(lh, jnp.concatenate([rh, rl], axis=1), NN)
    return both[:, 0:k] + (both[:, k:2 * k] + dot(ll, rh, NN))


def basis_kernel(
    high_ref, low_ref, cov_high, cov_low, shift_ref, gram_ref, start_ref, masked_ref,
    loadings_hbm, scores_hbm, explained_ref, loadings_ref, scores_ref, basis_ref, inverse_ref, lsem, ssem,
):
    var = lax.axis_index("var")
    local_vars = masked_ref.shape[0]
    width = local_vars * M
    k = start_ref.shape[1]
    basis_ref[...] = start_ref[...]

    def sweep(_, carry):
        image = packed((cov_high[...], cov_low[...]), split(basis_ref[...]))
        gram = dot(image, image, TN, HIGHEST)
        for i, tile in enumerate(inverse_factor(gram)):
            inverse_ref[8 * i:8 * i + 8, :] = tile
        basis_ref[...] = dot(image, inverse_ref[...], NT, HIGHEST)
        return carry

    lax.fori_loop(0, SWEEPS, sweep, 0)

    own = pl.ds(pl.multiple_of(var * width, width), width)
    basis_low = basis_ref[own, :].astype(BF16)
    mine = [basis_low[v * M:(v + 1) * M, :] for v in range(local_vars)]
    flush = []
    for v in range(local_vars):
        loadings_ref[v] = dot(mine[v], masked_ref[v], TN).astype(BF16)
        flush.append(pltpu.make_async_copy(loadings_ref.at[v], loadings_hbm.at[v], lsem.at[v]))
        flush[v].start()

    offset = shift_ref[0:1, :]
    tall = jnp.where(lax.broadcasted_iota(jnp.int32, (8, offset.shape[1]), 0) == 0, offset, 0.0)
    scores = packed((high_ref[...], low_ref[...]), split(basis_ref[...])) - dot(tall, basis_ref[...], NN, HIGHEST)[0:1, :]
    scores_ref[...] = scores
    flush.append(pltpu.make_async_copy(scores_ref, scores_hbm, ssem))
    flush[-1].start()

    scores_low = scores.astype(BF16)
    wide = basis_low.astype(F32)
    zero = jnp.zeros((M, k), F32)
    spread, quads = [], []
    for v in range(local_vars):
        line = wide[v * M:(v + 1) * M, :]
        spread.append(jnp.concatenate([2.0 * line if u == v else zero for u in range(local_vars)], axis=1))
        inner = dot(gram_ref[:, v * M:(v + 1) * M], line, NN, HIGHEST)
        quads.append(dot(line, inner, TN, HIGHEST))
    cross = jnp.concatenate(spread, axis=0)
    square = split(-jnp.concatenate(quads, axis=1))
    right = jnp.concatenate([cross.astype(BF16), cross.astype(BF16), square[0], square[1]], axis=0)
    left = jnp.concatenate([high_ref[:, own], low_ref[:, own], scores_low, scores_low], axis=1)
    tall = jnp.where(lax.broadcasted_iota(jnp.int32, (8, width), 0) == 0, shift_ref[0:1, own], 0.0)
    inside = dot(left, right, NN) - dot(tall, cross, NN, HIGHEST)[0:1, :]
    ones = jnp.ones((16, k), BF16)
    scores_wide = scores_low.astype(F32)
    for v in range(local_vars):
        gain = split(scores_wide * inside[:, v * k:(v + 1) * k])
        summed = (dot(ones, gain[0], NT) + dot(ones, gain[1], NT)) / M
        explained_ref[v:v + 1, :] = summed[0:1, :]
    for copy in flush:
        copy.wait()


def finish(high, low, cov_high, cov_low, shift, gram, start, masked):
    local_vars, _, points = masked.shape
    samples, joint = high.shape
    k = start.shape[1]
    return pl.pallas_call(
        basis_kernel,
        out_shape=(
            jax.ShapeDtypeStruct((local_vars, k, points), BF16),
            jax.ShapeDtypeStruct((samples, k), F32),
            jax.ShapeDtypeStruct((local_vars, samples), F32),
        ),
        in_specs=[pl.BlockSpec(memory_space=pltpu.VMEM)] * 8,
        out_specs=(
            pl.BlockSpec(memory_space=pltpu.HBM),
            pl.BlockSpec(memory_space=pltpu.HBM),
            pl.BlockSpec(memory_space=pltpu.VMEM),
        ),
        scratch_shapes=[
            pltpu.VMEM((local_vars, k, points), BF16),
            pltpu.VMEM((samples, k), F32),
            pltpu.VMEM((joint, k), F32),
            pltpu.VMEM((k, k), F32),
            pltpu.SemaphoreType.DMA((local_vars,)),
            pltpu.SemaphoreType.DMA(()),
        ],
        compiler_params=pltpu.CompilerParams(vmem_limit_bytes=48 * 1024 * 1024),
        name="finish",
    )(high, low, cov_high, cov_low, shift, gram, start, masked)


def shards(n, nv, fields, eigenfunctions, start, grid_count):
    high, low, cov_high, cov_low, shift, gram, masked = gather_scores(n, nv, grid_count, fields, eigenfunctions)
    return finish(high, low, cov_high, cov_low, shift, gram, start, masked)


def solution(mesh):
    return jax.shard_map(
        functools.partial(shards, mesh.shape["space"], mesh.shape["var"]),
        mesh=mesh,
        in_specs=(P("var", None, "space"), P("var", None, "space"), P(), P()),
        out_specs=(P("var", None, "space"), P(), P("var", None)),
        check_vma=False,
    )
```

```python
import functools

import jax
import jax.numpy as jnp
from jax import lax
from jax.experimental import pallas as pl
from jax.experimental.pallas import tpu as pltpu
from jax.sharding import PartitionSpec as P

M = 64
SWEEPS = 2
MESH = pl.DeviceIdType.MESH
F32 = jnp.float32
BF16 = jnp.bfloat16
HIGHEST = lax.Precision.HIGHEST


def dot(left, right, dims, precision=None):
    return lax.dot_general(left, right, (dims, ((), ())), precision=precision, preferred_element_type=F32)


NN = ((1,), (0,))
NT = ((1,), (1,))
TN = ((0,), (0,))


def split(x):
    high = x.astype(BF16)
    return high, (x - high.astype(F32)).astype(BF16)


def dot3(left, right, dims):
    (lh, ll), (rh, rl) = left, right
    return dot(lh, rh, dims) + (dot(lh, rl, dims) + dot(ll, rh, dims))


def remote(src, dst, send, recv, target):
    return pltpu.make_async_remote_copy(
        src_ref=src, dst_ref=dst, send_sem=send, recv_sem=recv, device_id=target, device_id_type=MESH
    )


def masked_block(count, eigen, first):
    points = first + lax.broadcasted_iota(jnp.int32, (1, eigen.shape[1]), 1)
    return eigen * jnp.where(points < count, 1.0, 0.0).astype(eigen.dtype)


SHARES = (4, 4, 4, 2, 2)
AHEAD = 4


def layout(samples):
    unit = samples // (4 * sum(SHARES))
    rows = [unit * share for share in SHARES]
    return rows, [sum(rows[:p]) for p in range(len(rows))]


def gather_kernel(
    n, counts_hbm, fields, eigen_hbm, high_ref, low_ref, cov_high, cov_low, shift_ref, gram_ref, masked_ref,
    counts, eigen, moment, fbuf, weights, part, rbuf, cross, jbuf, gpart, grbuf, gred, gfull,
    csem, esem, fsem, rsend, rrecv, xsend, xrecv, asend, arecv, psend, precv, gsend, grecv, hsend, hrecv,
):
    var, me = lax.axis_index("var"), lax.axis_index("space")
    local_vars, samples, local_points = fields.shape
    rows, start = layout(samples)
    pieces = len(rows)
    chunk = 2 * rows[0]
    full = sum(size == rows[0] for size in rows)
    width = local_vars * M
    groups = n // 4
    side, core = var // 2, lax.rem(var, 2)
    group, quad = me // 4, lax.rem(me, 4)
    depth, lane_y = quad // 2, lax.rem(quad, 2)
    far, mate = 1 - side, 1 - core

    def owner(dz, dy):
        return 2 * (depth + dz - 2 * depth * dz) + lane_y + dy - 2 * lane_y * dy

    def fetch(i):
        swapped = 2 * (i // 2) + lax.rem(depth + 1 + i, 2)
        first = chunk * jnp.where(i < 2 * full, swapped, i)
        block = pl.ds(pl.multiple_of(first, chunk), chunk)
        return pltpu.make_async_copy(fields.at[:, block, :], fbuf.at[i], fsem.at[i])

    eigen_copy = pltpu.make_async_copy(eigen_hbm, eigen, esem)
    counts_copy = pltpu.make_async_copy(counts_hbm, counts, csem)
    counts_copy.start()
    eigen_copy.start()
    for i in range(min(2, samples // chunk)):
        fetch(i).start()

    xside, yside, zside = (2 * far + mate, me), (2 * side + mate, 4 * group + owner(0, 1)), (2 * side + mate, 4 * group + owner(1, 0))
    corner, partner = (2 * far + mate, 4 * group + owner(1, 1)), (2 * side + mate, me)
    barrier = pltpu.get_barrier_semaphore()
    for d in range(1, n):
        pl.semaphore_signal(barrier, inc=1, device_id=(var, lax.rem(me + d, n)), device_id_type=MESH)
    for target in (xside, yside, zside, corner, partner):
        pl.semaphore_signal(barrier, inc=1, device_id=target, device_id_type=MESH)

    counts_copy.wait()
    eigen_copy.wait()
    for i in range(2, min(AHEAD, samples // chunk)):
        fetch(i).start()
    for v in range(local_vars):
        masked = masked_block(counts[var * local_vars + v], eigen[v], me * local_points)
        masked_ref[v] = masked
        weights[v * M:(v + 1) * M, :] = masked

    pl.semaphore_wait(barrier, n - 1 + 5)

    def span(p, o):
        return pl.ds(pl.multiple_of(4 * start[p] + o * rows[p], 8), rows[p])

    def send_part(p, k):
        o = owner(1 - k // 2, 1 - k % 2)
        if isinstance(p, int):
            source = part.at[span(p, o)]
            slot = rbuf.at[pl.ds(3 * start[p] + k * rows[p], rows[p])]
        else:
            source = part.at[pl.ds(pl.multiple_of((4 * p + o) * rows[0], 8), rows[0])]
            slot = rbuf.at[pl.ds(pl.multiple_of((3 * p + k) * rows[0], 8), rows[0])]
        j = 3 * p + k
        return remote(source, slot, rsend.at[j], rrecv.at[j], (var, 4 * group + o))

    column = lax.broadcasted_iota(jnp.int32, (chunk, width), 1) // M

    def project(i, first):
        later = i + AHEAD
        if not isinstance(i, int):
            pl.when(later < samples // chunk)(lambda: fetch(later).start())
        elif later < samples // chunk:
            fetch(later).start()
        fetch(i).wait()
        scores = dot(fbuf[i, 0], weights[...], NT)
        for v in range(1, local_vars):
            scores = jnp.where(column == v, dot(fbuf[i, v], weights[...], NT), scores)
        part[pl.ds(pl.multiple_of(first, chunk), chunk), :] = scores

    def step(p, carry):
        @pl.when(p > 0)
        def _():
            send_part(p - 1, 2).start()

        project(2 * p, chunk * (2 * p + 1 - depth))
        send_part(p, 0).start()
        send_part(p, 1).start()
        project(2 * p + 1, chunk * (2 * p + depth))
        return carry

    def block(p, origin, o):
        return jbuf.at[origin, span(p, o)]

    own = [block(p, var, quad) for p in range(pieces)]

    def held(p):
        return pl.ds(start[p], rows[p])

    def send_cross(p, d):
        j = p * (groups - 1) + d - 1
        target = (var, 4 * lax.rem(group + d, groups) + quad)
        return remote(cross.at[group, held(p)], cross.at[group, held(p)], xsend.at[j], xrecv.at[j], target)

    def half_sum(p):
        total = part[span(p, quad), :]
        for k in range(3):
            send_part(p, k).wait_recv()
            first = 3 * start[p] + k * rows[p]
            total = total + rbuf[first:first + rows[p], :]
        cross[group, held(p)] = total
        for d in range(1, groups):
            send_cross(p, d).start()

    def relation(p, kind):
        return {
            "x": lambda: block(p, 2 * far + mate, quad),
            "y": lambda: block(p, 2 * side + mate, owner(0, 1)),
            "z": lambda: block(p, 2 * side + mate, owner(1, 0)),
            "xy": lambda: block(p, 2 * far + core, owner(0, 1)),
            "xz": lambda: block(p, 2 * far + core, owner(1, 0)),
            "yz": lambda: block(p, 2 * side + core, owner(1, 1)),
            "xyz": lambda: block(p, 2 * far + mate, owner(1, 1)),
        }[kind]()

    kinds = ("x", "y", "z", "xy", "xz", "yz", "xyz")

    def route(p, kind):
        last = ("yz", xside) if p == 0 else ("", corner)
        return {
            "x": ("", xside), "y": ("", yside), "z": ("", zside),
            "xz": ("x", zside), "xy": ("y", xside), "yz": ("z", yside), "xyz": last,
        }[kind]

    def send_on(p, kind):
        source, target = route(p, kind)
        piece = own[p] if source == "" else relation(p, source)
        j = p * 7 + kinds.index(kind)
        return remote(piece, piece, asend.at[j], arecv.at[j], target)

    def share(p, kind):
        piece = own[p] if kind == "" else relation(p, kind)
        j = p * 8 + (7 if kind == "" else kinds.index(kind))
        return remote(piece, piece, psend.at[j], precv.at[j], partner)

    def arrived(p, kind):
        send_on(p, kind).wait_recv()
        for other in kinds:
            if route(p, other)[0] == kind:
                send_on(p, other).start()
        share(p, kind).start()

    def full_sum(p):
        for d in range(1, groups):
            send_cross(p, d).wait_recv()
        total = cross[0, held(p)]
        for g in range(1, groups):
            total = total + cross[g, held(p)]
        own[p][...] = total
        for kind in kinds:
            if route(p, kind)[0] == "":
                send_on(p, kind).start()
        share(p, "").start()

    def first_hop(p):
        for kind in ("x", "y", "z"):
            arrived(p, kind)

    def second_hop(p):
        for kind in ("xy", "xz", "yz"):
            arrived(p, kind)

    def third_hop(p):
        arrived(p, "xyz")

    def moments(first, last, initial):
        for p in range(first, last + 1):
            for kind in kinds + ("",):
                share(p, kind).wait_recv()
        place = slice(4 * start[first], 4 * (start[last] + rows[last]))
        block = jnp.concatenate([jbuf[v, place, :] for v in range(jbuf.shape[0])], axis=1)
        if initial:
            shift_ref[0:1, :] = jnp.sum(block, axis=0, keepdims=True) / block.shape[0]
        block = block - shift_ref[0:1, :]
        total = jnp.sum(block, axis=0, keepdims=True)
        high, low = split(block)
        high_ref[place, :] = high
        low_ref[place, :] = low
        square = dot3((high, low), (high, low), TN)
        shift_ref[1:2, :] = total if initial else shift_ref[1:2, :] + total
        moment[...] = square if initial else moment[...] + square

    grows = M // n

    def send_gram(d):
        target = lax.rem(me + d, n)
        return remote(gpart.at[target], grbuf.at[d - 1], gsend.at[d - 1], grecv.at[d - 1], (var, target))

    def send_gfull(d):
        return remote(gred, gfull.at[me], hsend.at[d - 1], hrecv.at[d - 1], (var, lax.rem(me + d, n)))

    def gram_parts():
        grams = [dot(masked_ref[v], masked_ref[v], NT) for v in range(local_vars)]
        gram = jnp.concatenate(grams, axis=1)
        gpart[...] = jnp.zeros_like(gpart)
        for s in range(n):
            gpart[s, 0:grows, :] = gram[s * grows:(s + 1) * grows, :]
        for d in range(1, n):
            send_gram(d).start()

    def gram_sum():
        gtotal = gpart[me]
        for d in range(1, n):
            send_gram(d).wait()
            gtotal = gtotal + grbuf[d - 1]
        gred[...] = gtotal
        gfull[me] = gtotal
        for d in range(1, n):
            send_gfull(d).start()

    lax.fori_loop(0, full, step, 0)
    send_part(full - 1, 2).start()
    half_sum(0)
    for p in range(full, pieces):
        project(full + p, chunk * (full + p))
        for k in range(3):
            send_part(p, k).start()
    gram_parts()
    order = (
        (0, 1), (0, 2), (0, 3), (0, 4), (1, 0), (1, 1), (2, 0), (1, 2), (1, 3), (1, 4), (5, 0), (2, 1), (3, 0),
        (2, 2), (2, 3), (2, 4), (3, 1), (4, 1), (4, 0), (3, 2), (4, 2), (3, 3), (4, 3), (3, 4), (4, 4),
    )
    for stage, p in order:
        if stage == 5:
            gram_sum()
        else:
            (half_sum, full_sum, first_hop, second_hop, third_hop)[stage](p)
    moments(1, 1, True)
    moments(0, 0, False)
    moments(2, 2, False)
    moments(3, 4, False)

    for d in range(1, n):
        send_gfull(d).wait()
    for p in range(pieces):
        for k in range(3):
            send_part(p, k).wait_send()
        for d in range(1, groups):
            send_cross(p, d).wait_send()
        for kind in kinds:
            send_on(p, kind).wait_send()
        for kind in kinds + ("",):
            share(p, kind).wait_send()

    offset = shift_ref[1:2, :] / samples
    shift_ref[0:1, :] = offset
    tall = jnp.where(lax.broadcasted_iota(jnp.int32, (16, offset.shape[1]), 0) == 0, offset, 0.0)
    outer = split(tall)
    cov = (moment[...] - samples * dot3(outer, outer, TN)) / (samples - 1)
    cov_high[...], cov_low[...] = split(cov)
    for s in range(n):
        gram_ref[s * grows:(s + 1) * grows, :] = gfull[s, 0:grows, :]


def gather_scores(n, nv, counts, fields, eigen):
    local_vars, samples, points = fields.shape
    rows, _ = layout(samples)
    pieces = len(rows)
    if nv != 4 or n % 4 or samples % (64 * sum(SHARES)):
        raise ValueError("unsupported mesh")
    chunk = 2 * rows[0]
    quarter = samples // 4
    width = local_vars * M
    groups = n // 4
    dma = pltpu.SemaphoreType.DMA
    pairs = [3 * pieces, max(1, pieces * (groups - 1)), 7 * pieces, 8 * pieces, n - 1, n - 1]
    return pl.pallas_call(
        functools.partial(gather_kernel, n),
        out_shape=(
            jax.ShapeDtypeStruct((samples, nv * width), BF16),
            jax.ShapeDtypeStruct((samples, nv * width), BF16),
            jax.ShapeDtypeStruct((nv * width, nv * width), BF16),
            jax.ShapeDtypeStruct((nv * width, nv * width), BF16),
            jax.ShapeDtypeStruct((8, nv * width), F32),
            jax.ShapeDtypeStruct((M, width), F32),
            jax.ShapeDtypeStruct((local_vars, M, points), BF16),
        ),
        in_specs=[pl.BlockSpec(memory_space=pltpu.HBM)] * 3,
        out_specs=(pl.BlockSpec(memory_space=pltpu.VMEM),) * 7,
        scratch_shapes=[
            pltpu.SMEM(counts.shape, jnp.int32),
            pltpu.VMEM((local_vars, M, points), BF16),
            pltpu.VMEM((nv * width, nv * width), F32),
            pltpu.VMEM((samples // chunk, local_vars, chunk, points), BF16),
            pltpu.VMEM((width, points), BF16),
            pltpu.VMEM((samples, width), F32),
            pltpu.VMEM((3 * quarter, width), F32),
            pltpu.VMEM((groups, quarter, width), F32),
            pltpu.VMEM((nv, samples, width), F32),
            pltpu.VMEM((n, 8, width), F32),
            pltpu.VMEM((n - 1, 8, width), F32),
            pltpu.VMEM((8, width), F32),
            pltpu.VMEM((n, 8, width), F32),
            dma(()),
            dma(()),
            dma((samples // chunk,)),
            *[dma((count,)) for count in pairs for _ in range(2)],
        ],
        compiler_params=pltpu.CompilerParams(
            collective_id=0, has_side_effects=True, vmem_limit_bytes=48 * 1024 * 1024
        ),
        name="gather_scores",
    )(*(pltpu.with_memory_space_constraint(x, pltpu.HBM) for x in (counts, fields, eigen)))


def inverse_factor(gram):
    size = gram.shape[0]
    tiles = size // 8
    rows = [gram[8 * i:8 * i + 8, :] for i in range(tiles)]
    lane = lax.broadcasted_iota(jnp.int32, (8, size), 1)
    sublane = lax.broadcasted_iota(jnp.int32, (8, size), 0)

    def columns(tile, b):
        return [jnp.broadcast_to(tile[:, 8 * b + j:8 * b + j + 1], (8, size)) for j in range(8)]

    def spread(tile, j):
        return jnp.broadcast_to(tile[j:j + 1, :], (8, size))

    done, top = [], []
    half = tiles // 2
    block = columns(rows[0], 0)
    for b in range(tiles):
        limit = half if b < half else tiles
        if b == half:
            upper = jnp.concatenate(top, axis=0)
            update = dot(upper[:, 8 * half:], upper, TN, HIGHEST)
            for i in range(half, tiles):
                rows[i] = jnp.where(lane < 8 * half, 0.0, rows[i]) - update[8 * (i - half):8 * (i - half) + 8, :]
            block = columns(rows[b], b)
        inside = (lane >= 8 * b) & (lane < 8 * b + 8)
        work = jnp.where(inside, jnp.where(lane - 8 * b == sublane, 1.0, 0.0), rows[b])
        inverse, cross, lower = [], {}, []
        pivot = None
        for j in range(8):
            diagonal = spread(block[j], j)
            pivot = diagonal if j == 0 else jnp.where(sublane == j, diagonal, pivot)
            inverse.append(1.0 / diagonal)
            for q in range(j + 1, 8):
                cross[j, q] = spread(block[j], q)
            if j == 7:
                break
            block[j + 1] = block[j + 1] - (block[j] * cross[j, j + 1]) * inverse[j]
            factor = block[j] * inverse[j]
            lower.append(factor)
            for q in range(j + 2, 8):
                block[q] = block[q] - factor * cross[j, q]
            work = work - jnp.where(sublane > j, factor, 0.0) * spread(work, j)
        scaled = work * lax.rsqrt(pivot)
        top.append(jnp.where((lane < 8 * b + 8) | (lane >= 8 * half), scaled, 0.0))
        done.append(jnp.where(lane < 8 * b + 8, scaled, 0.0))
        if b + 1 == limit:
            continue
        line = [spread(work, j) for j in range(8)]
        for i in range(b + 1, min(b + 3, limit)):
            value, factors = columns(rows[i], b), []
            for j in range(8):
                factors.append(value[j] * inverse[j])
                for q in range(j + 1, 8):
                    value[q] = value[q] - factors[j] * cross[j, q]
            if i == b + 1:
                block = columns(rows[i], i)
                for q in range(8):
                    for j in range(8):
                        block[q] = block[q] - factors[j] * spread(value[j], q)
            new = jnp.where(inside, 0.0, rows[i])
            for j in range(8):
                new = new - factors[j] * line[j]
            rows[i] = new
        if b + 3 >= limit:
            continue
        solved = [None] * 8
        for j in reversed(range(8)):
            value = line[j] * inverse[j]
            for q in range(j + 1, 8):
                value = value - spread(lower[j], q) * solved[q]
            solved[j] = value
        for i in range(b + 3, limit):
            new = jnp.where(inside, 0.0, rows[i])
            entry = columns(rows[i], b)
            for j in range(8):
                new = new - entry[j] * solved[j]
            rows[i] = new
    return done


def basis_kernel(
    high_ref, low_ref, cov_high, cov_low, shift_ref, gram_ref, start_ref, masked_ref,
    loadings_hbm, scores_hbm, explained_ref, loadings_ref, scores_ref, basis_ref, inverse_ref, lsem, ssem,
):
    var = lax.axis_index("var")
    local_vars = masked_ref.shape[0]
    width = local_vars * M
    k = start_ref.shape[1]
    basis_ref[...] = start_ref[...].T

    def sweep(_, carry):
        high, low = split(basis_ref[...])
        both = dot(jnp.concatenate([high, low], axis=0), cov_high[...], NN)
        image = both[0:k] + (both[k:2 * k] + dot(high, cov_low[...], NN))
        gram = dot(image, image, NT, HIGHEST)
        for i, tile in enumerate(inverse_factor(gram)):
            inverse_ref[8 * i:8 * i + 8, :] = tile
        basis_ref[...] = dot(inverse_ref[...], image, NN, HIGHEST)
        return carry

    lax.fori_loop(0, SWEEPS, sweep, 0)

    own = pl.ds(pl.multiple_of(var * width, width), width)
    mine = basis_ref[:, own].astype(BF16)
    flush = []
    for v in range(local_vars):
        loadings_ref[v] = dot(mine[:, v * M:(v + 1) * M], masked_ref[v], NN).astype(BF16)
        flush.append(pltpu.make_async_copy(loadings_ref.at[v], loadings_hbm.at[v], lsem.at[v]))
        flush[v].start()

    high, low = split(basis_ref[...])
    offset = shift_ref[0:1, :]
    tall = jnp.where(lax.broadcasted_iota(jnp.int32, (8, offset.shape[1]), 0) == 0, offset, 0.0)
    both = dot(high_ref[...], jnp.concatenate([high, low], axis=0), NT)
    mean = dot(tall, basis_ref[...], NT, HIGHEST)[0:1, :]
    scores = both[:, 0:k] + (both[:, k:2 * k] + dot(low_ref[...], high, NT)) - mean
    scores_ref[...] = scores
    flush.append(pltpu.make_async_copy(scores_ref, scores_hbm, ssem))
    flush[-1].start()

    scores_low = scores.astype(BF16)
    wide = mine.astype(F32)
    owner = lax.broadcasted_iota(jnp.int32, (k, width), 1) // M
    spread, quads = [], []
    for v in range(local_vars):
        line = wide[:, v * M:(v + 1) * M]
        spread.append(jnp.where(owner == v, 2.0 * wide, 0.0))
        inner = dot(line, gram_ref[:, v * M:(v + 1) * M], NN, HIGHEST)
        quads.append(dot(inner, line, NT, HIGHEST))
    cross = jnp.concatenate(spread, axis=0)
    square = split(-jnp.concatenate(quads, axis=0))
    right = jnp.concatenate([cross.astype(BF16), cross.astype(BF16), square[0], square[1]], axis=1)
    left = jnp.concatenate([high_ref[:, own], low_ref[:, own], scores_low, scores_low], axis=1)
    tall = jnp.where(lax.broadcasted_iota(jnp.int32, (8, width), 0) == 0, shift_ref[0:1, own], 0.0)
    inside = dot(left, right, NT) - dot(tall, cross, NT, HIGHEST)[0:1, :]
    ones = jnp.ones((16, k), BF16)
    scores_wide = scores_low.astype(F32)
    for v in range(local_vars):
        gain = split(scores_wide * inside[:, v * k:(v + 1) * k])
        summed = (dot(ones, gain[0], NT) + dot(ones, gain[1], NT)) / M
        explained_ref[v:v + 1, :] = summed[0:1, :]
    for copy in flush:
        copy.wait()


def finish(high, low, cov_high, cov_low, shift, gram, start, masked):
    local_vars, _, points = masked.shape
    samples, joint = high.shape
    k = start.shape[1]
    return pl.pallas_call(
        basis_kernel,
        out_shape=(
            jax.ShapeDtypeStruct((local_vars, k, points), BF16),
            jax.ShapeDtypeStruct((samples, k), F32),
            jax.ShapeDtypeStruct((local_vars, samples), F32),
        ),
        in_specs=[pl.BlockSpec(memory_space=pltpu.VMEM)] * 8,
        out_specs=(
            pl.BlockSpec(memory_space=pltpu.HBM),
            pl.BlockSpec(memory_space=pltpu.HBM),
            pl.BlockSpec(memory_space=pltpu.VMEM),
        ),
        scratch_shapes=[
            pltpu.VMEM((local_vars, k, points), BF16),
            pltpu.VMEM((samples, k), F32),
            pltpu.VMEM((k, joint), F32),
            pltpu.VMEM((k, k), F32),
            pltpu.SemaphoreType.DMA((local_vars,)),
            pltpu.SemaphoreType.DMA(()),
        ],
        compiler_params=pltpu.CompilerParams(vmem_limit_bytes=48 * 1024 * 1024),
        name="finish",
    )(high, low, cov_high, cov_low, shift, gram, start, masked)


def shards(n, nv, fields, eigenfunctions, start, grid_count):
    high, low, cov_high, cov_low, shift, gram, masked = gather_scores(n, nv, grid_count, fields, eigenfunctions)
    return finish(high, low, cov_high, cov_low, shift, gram, start, masked)


def solution(mesh):
    return jax.shard_map(
        functools.partial(shards, mesh.shape["space"], mesh.shape["var"]),
        mesh=mesh,
        in_specs=(P("var", None, "space"), P("var", None, "space"), P(), P()),
        out_specs=(P("var", None, "space"), P(), P("var", None)),
        check_vma=False,
    )
```

```python
import functools

import jax
import jax.numpy as jnp
from jax import lax
from jax.experimental import pallas as pl
from jax.experimental.pallas import tpu as pltpu
from jax.sharding import PartitionSpec as P

M = 64
SWEEPS = 2
MESH = pl.DeviceIdType.MESH
F32 = jnp.float32
BF16 = jnp.bfloat16
HIGHEST = lax.Precision.HIGHEST


def dot(left, right, dims, precision=None):
    return lax.dot_general(left, right, (dims, ((), ())), precision=precision, preferred_element_type=F32)


NN = ((1,), (0,))
NT = ((1,), (1,))
TN = ((0,), (0,))


def split(x):
    high = x.astype(BF16)
    return high, (x - high.astype(F32)).astype(BF16)


def dot3(left, right, dims):
    (lh, ll), (rh, rl) = left, right
    return dot(lh, rh, dims) + (dot(lh, rl, dims) + dot(ll, rh, dims))


def remote(src, dst, send, recv, target):
    return pltpu.make_async_remote_copy(
        src_ref=src, dst_ref=dst, send_sem=send, recv_sem=recv, device_id=target, device_id_type=MESH
    )


def masked_block(count, eigen, first):
    points = first + lax.broadcasted_iota(jnp.int32, (1, eigen.shape[1]), 1)
    return eigen * jnp.where(points < count, 1.0, 0.0).astype(eigen.dtype)


SHARES = (4, 4, 4, 2, 2)
AHEAD = 4


def layout(samples):
    unit = samples // (4 * sum(SHARES))
    rows = [unit * share for share in SHARES]
    return rows, [sum(rows[:p]) for p in range(len(rows))]


def gather_kernel(
    n, counts_hbm, fields, eigen_hbm, high_ref, low_ref, cov_high, cov_low, shift_ref, gram_ref, masked_ref,
    counts, eigen, moment, fbuf, weights, part, rbuf, cross, jbuf, gpart, grbuf, gred, gfull,
    csem, esem, fsem, rsend, rrecv, xsend, xrecv, asend, arecv, psend, precv, gsend, grecv, hsend, hrecv,
):
    var, me = lax.axis_index("var"), lax.axis_index("space")
    local_vars, samples, local_points = fields.shape
    rows, start = layout(samples)
    pieces = len(rows)
    chunk = 2 * rows[0]
    full = sum(size == rows[0] for size in rows)
    width = local_vars * M
    groups = n // 4
    side, core = var // 2, lax.rem(var, 2)
    group, quad = me // 4, lax.rem(me, 4)
    depth, lane_y = quad // 2, lax.rem(quad, 2)
    far, mate = 1 - side, 1 - core

    def owner(dz, dy):
        return 2 * (depth + dz - 2 * depth * dz) + lane_y + dy - 2 * lane_y * dy

    def fetch(i):
        swapped = 2 * (i // 2) + lax.rem(depth + 1 + i, 2)
        first = chunk * jnp.where(i < 2 * full, swapped, i)
        block = pl.ds(pl.multiple_of(first, chunk), chunk)
        return pltpu.make_async_copy(fields.at[:, block, :], fbuf.at[i], fsem.at[i])

    eigen_copy = pltpu.make_async_copy(eigen_hbm, eigen, esem)
    counts_copy = pltpu.make_async_copy(counts_hbm, counts, csem)
    counts_copy.start()
    eigen_copy.start()
    for i in range(min(2, samples // chunk)):
        fetch(i).start()

    xside, yside, zside = (2 * far + mate, me), (2 * side + mate, 4 * group + owner(0, 1)), (2 * side + mate, 4 * group + owner(1, 0))
    corner, partner = (2 * far + mate, 4 * group + owner(1, 1)), (2 * side + mate, me)
    barrier = pltpu.get_barrier_semaphore()
    for d in range(1, n):
        pl.semaphore_signal(barrier, inc=1, device_id=(var, lax.rem(me + d, n)), device_id_type=MESH)
    for target in (xside, yside, zside, corner, partner):
        pl.semaphore_signal(barrier, inc=1, device_id=target, device_id_type=MESH)

    counts_copy.wait()
    eigen_copy.wait()
    for i in range(2, min(AHEAD, samples // chunk)):
        fetch(i).start()
    for v in range(local_vars):
        masked = masked_block(counts[var * local_vars + v], eigen[v], me * local_points)
        masked_ref[v] = masked
        weights[v * M:(v + 1) * M, :] = masked

    pl.semaphore_wait(barrier, n - 1 + 5)

    def span(p, o):
        return pl.ds(pl.multiple_of(4 * start[p] + o * rows[p], 8), rows[p])

    def send_part(p, k):
        o = owner(1 - k // 2, 1 - k % 2)
        if isinstance(p, int):
            source = part.at[span(p, o)]
            slot = rbuf.at[pl.ds(3 * start[p] + k * rows[p], rows[p])]
        else:
            source = part.at[pl.ds(pl.multiple_of((4 * p + o) * rows[0], 8), rows[0])]
            slot = rbuf.at[pl.ds(pl.multiple_of((3 * p + k) * rows[0], 8), rows[0])]
        j = 3 * p + k
        return remote(source, slot, rsend.at[j], rrecv.at[j], (var, 4 * group + o))

    column = lax.broadcasted_iota(jnp.int32, (chunk, width), 1) // M

    def project(i, first):
        later = i + AHEAD
        if not isinstance(i, int):
            pl.when(later < samples // chunk)(lambda: fetch(later).start())
        elif later < samples // chunk:
            fetch(later).start()
        fetch(i).wait()
        scores = dot(fbuf[i, 0], weights[...], NT)
        for v in range(1, local_vars):
            scores = jnp.where(column == v, dot(fbuf[i, v], weights[...], NT), scores)
        part[pl.ds(pl.multiple_of(first, chunk), chunk), :] = scores

    def step(p, carry):
        @pl.when(p > 0)
        def _():
            send_part(p - 1, 2).start()

        project(2 * p, chunk * (2 * p + 1 - depth))
        send_part(p, 0).start()
        send_part(p, 1).start()
        project(2 * p + 1, chunk * (2 * p + depth))
        return carry

    def block(p, origin, o):
        return jbuf.at[origin, span(p, o)]

    own = [block(p, var, quad) for p in range(pieces)]

    def held(p):
        return pl.ds(start[p], rows[p])

    def send_cross(p, d):
        j = p * (groups - 1) + d - 1
        target = (var, 4 * lax.rem(group + d, groups) + quad)
        return remote(cross.at[group, held(p)], cross.at[group, held(p)], xsend.at[j], xrecv.at[j], target)

    def half_sum(p):
        total = part[span(p, quad), :]
        for k in range(3):
            send_part(p, k).wait_recv()
            first = 3 * start[p] + k * rows[p]
            total = total + rbuf[first:first + rows[p], :]
        cross[group, held(p)] = total
        for d in range(1, groups):
            send_cross(p, d).start()

    def relation(p, kind):
        return {
            "x": lambda: block(p, 2 * far + mate, quad),
            "y": lambda: block(p, 2 * side + mate, owner(0, 1)),
            "z": lambda: block(p, 2 * side + mate, owner(1, 0)),
            "xy": lambda: block(p, 2 * far + core, owner(0, 1)),
            "xz": lambda: block(p, 2 * far + core, owner(1, 0)),
            "yz": lambda: block(p, 2 * side + core, owner(1, 1)),
            "xyz": lambda: block(p, 2 * far + mate, owner(1, 1)),
        }[kind]()

    kinds = ("x", "y", "z", "xy", "xz", "yz", "xyz")

    def route(p, kind):
        last = ("yz", xside) if p == 0 else ("", corner)
        return {
            "x": ("", xside), "y": ("", yside), "z": ("", zside),
            "xz": ("x", zside), "xy": ("y", xside), "yz": ("z", yside), "xyz": last,
        }[kind]

    def send_on(p, kind):
        source, target = route(p, kind)
        piece = own[p] if source == "" else relation(p, source)
        j = p * 7 + kinds.index(kind)
        return remote(piece, piece, asend.at[j], arecv.at[j], target)

    def share(p, kind):
        piece = own[p] if kind == "" else relation(p, kind)
        j = p * 8 + (7 if kind == "" else kinds.index(kind))
        return remote(piece, piece, psend.at[j], precv.at[j], partner)

    def arrived(p, kind):
        send_on(p, kind).wait_recv()
        for other in kinds:
            if route(p, other)[0] == kind:
                send_on(p, other).start()
        share(p, kind).start()

    def full_sum(p):
        for d in range(1, groups):
            send_cross(p, d).wait_recv()
        total = cross[0, held(p)]
        for g in range(1, groups):
            total = total + cross[g, held(p)]
        own[p][...] = total
        for kind in reversed(kinds):
            if route(p, kind)[0] == "":
                send_on(p, kind).start()
        share(p, "").start()

    def first_hop(p):
        for kind in ("x", "y", "z"):
            arrived(p, kind)

    def second_hop(p):
        for kind in ("xy", "xz", "yz"):
            arrived(p, kind)

    def third_hop(p):
        arrived(p, "xyz")

    def moments(first, last, initial):
        for p in range(first, last + 1):
            for kind in kinds + ("",):
                share(p, kind).wait_recv()
        place = slice(4 * start[first], 4 * (start[last] + rows[last]))
        block = jnp.concatenate([jbuf[v, place, :] for v in range(jbuf.shape[0])], axis=1)
        if initial:
            shift_ref[0:1, :] = jnp.sum(block, axis=0, keepdims=True) / block.shape[0]
        block = block - shift_ref[0:1, :]
        total = jnp.sum(block, axis=0, keepdims=True)
        high, low = split(block)
        high_ref[place, :] = high
        low_ref[place, :] = low
        square = dot3((high, low), (high, low), TN)
        shift_ref[1:2, :] = total if initial else shift_ref[1:2, :] + total
        moment[...] = square if initial else moment[...] + square

    grows = M // n

    def send_gram(d):
        target = lax.rem(me + d, n)
        return remote(gpart.at[target], grbuf.at[d - 1], gsend.at[d - 1], grecv.at[d - 1], (var, target))

    def send_gfull(d):
        return remote(gred, gfull.at[me], hsend.at[d - 1], hrecv.at[d - 1], (var, lax.rem(me + d, n)))

    def gram_parts():
        grams = [dot(masked_ref[v], masked_ref[v], NT) for v in range(local_vars)]
        gram = jnp.concatenate(grams, axis=1)
        gpart[...] = jnp.zeros_like(gpart)
        for s in range(n):
            gpart[s, 0:grows, :] = gram[s * grows:(s + 1) * grows, :]
        for d in range(1, n):
            send_gram(d).start()

    def gram_sum():
        gtotal = gpart[me]
        for d in range(1, n):
            send_gram(d).wait()
            gtotal = gtotal + grbuf[d - 1]
        gred[...] = gtotal
        gfull[me] = gtotal
        for d in range(1, n):
            send_gfull(d).start()

    lax.fori_loop(0, full, step, 0)
    send_part(full - 1, 2).start()
    half_sum(0)
    for p in range(full, pieces):
        project(full + p, chunk * (full + p))
        for k in range(3):
            send_part(p, k).start()
    order = (
        (0, 1), (0, 2), (5, 1), (0, 3), (0, 4), (1, 0), (1, 1), (2, 0), (1, 2), (1, 3), (1, 4), (5, 0), (2, 1), (3, 0),
        (2, 2), (2, 3), (2, 4), (3, 1), (4, 1), (4, 0), (3, 2), (4, 2), (3, 3), (4, 3), (3, 4), (4, 4),
    )
    for stage, p in order:
        if stage == 5:
            (gram_parts if p == 1 else gram_sum)()
        else:
            (half_sum, full_sum, first_hop, second_hop, third_hop)[stage](p)
    moments(1, 1, True)
    moments(0, 0, False)
    moments(2, 2, False)
    moments(3, 4, False)

    for d in range(1, n):
        send_gfull(d).wait()
    for p in range(pieces):
        for k in range(3):
            send_part(p, k).wait_send()
        for d in range(1, groups):
            send_cross(p, d).wait_send()
        for kind in kinds:
            send_on(p, kind).wait_send()
        for kind in kinds + ("",):
            share(p, kind).wait_send()

    offset = shift_ref[1:2, :] / samples
    shift_ref[0:1, :] = offset
    tall = jnp.where(lax.broadcasted_iota(jnp.int32, (16, offset.shape[1]), 0) == 0, offset, 0.0)
    outer = split(tall)
    cov = (moment[...] - samples * dot3(outer, outer, TN)) / (samples - 1)
    cov_high[...], cov_low[...] = split(cov)
    for s in range(n):
        gram_ref[s * grows:(s + 1) * grows, :] = gfull[s, 0:grows, :]


def gather_scores(n, nv, counts, fields, eigen):
    local_vars, samples, points = fields.shape
    rows, _ = layout(samples)
    pieces = len(rows)
    if nv != 4 or n % 4 or samples % (64 * sum(SHARES)):
        raise ValueError("unsupported mesh")
    chunk = 2 * rows[0]
    quarter = samples // 4
    width = local_vars * M
    groups = n // 4
    dma = pltpu.SemaphoreType.DMA
    pairs = [3 * pieces, max(1, pieces * (groups - 1)), 7 * pieces, 8 * pieces, n - 1, n - 1]
    return pl.pallas_call(
        functools.partial(gather_kernel, n),
        out_shape=(
            jax.ShapeDtypeStruct((samples, nv * width), BF16),
            jax.ShapeDtypeStruct((samples, nv * width), BF16),
            jax.ShapeDtypeStruct((nv * width, nv * width), BF16),
            jax.ShapeDtypeStruct((nv * width, nv * width), BF16),
            jax.ShapeDtypeStruct((8, nv * width), F32),
            jax.ShapeDtypeStruct((M, width), F32),
            jax.ShapeDtypeStruct((local_vars, M, points), BF16),
        ),
        in_specs=[pl.BlockSpec(memory_space=pltpu.HBM)] * 3,
        out_specs=(pl.BlockSpec(memory_space=pltpu.VMEM),) * 7,
        scratch_shapes=[
            pltpu.SMEM(counts.shape, jnp.int32),
            pltpu.VMEM((local_vars, M, points), BF16),
            pltpu.VMEM((nv * width, nv * width), F32),
            pltpu.VMEM((samples // chunk, local_vars, chunk, points), BF16),
            pltpu.VMEM((width, points), BF16),
            pltpu.VMEM((samples, width), F32),
            pltpu.VMEM((3 * quarter, width), F32),
            pltpu.VMEM((groups, quarter, width), F32),
            pltpu.VMEM((nv, samples, width), F32),
            pltpu.VMEM((n, 8, width), F32),
            pltpu.VMEM((n - 1, 8, width), F32),
            pltpu.VMEM((8, width), F32),
            pltpu.VMEM((n, 8, width), F32),
            dma(()),
            dma(()),
            dma((samples // chunk,)),
            *[dma((count,)) for count in pairs for _ in range(2)],
        ],
        compiler_params=pltpu.CompilerParams(
            collective_id=0, has_side_effects=True, vmem_limit_bytes=48 * 1024 * 1024
        ),
        name="gather_scores",
    )(*(pltpu.with_memory_space_constraint(x, pltpu.HBM) for x in (counts, fields, eigen)))


def inverse_factor(gram):
    size = gram.shape[0]
    tiles = size // 8
    rows = [gram[8 * i:8 * i + 8, :] for i in range(tiles)]
    lane = lax.broadcasted_iota(jnp.int32, (8, size), 1)
    sublane = lax.broadcasted_iota(jnp.int32, (8, size), 0)

    def columns(tile, b):
        return [jnp.broadcast_to(tile[:, 8 * b + j:8 * b + j + 1], (8, size)) for j in range(8)]

    def spread(tile, j):
        return jnp.broadcast_to(tile[j:j + 1, :], (8, size))

    done, top = [], []
    half = tiles // 2
    block = columns(rows[0], 0)
    for b in range(tiles):
        limit = half if b < half else tiles
        if b == half:
            upper = jnp.concatenate(top, axis=0)
            update = dot(upper[:, 8 * half:], upper, TN, HIGHEST)
            for i in range(half, tiles):
                rows[i] = jnp.where(lane < 8 * half, 0.0, rows[i]) - update[8 * (i - half):8 * (i - half) + 8, :]
            block = columns(rows[b], b)
        inside = (lane >= 8 * b) & (lane < 8 * b + 8)
        work = jnp.where(inside, jnp.where(lane - 8 * b == sublane, 1.0, 0.0), rows[b])
        inverse, cross, lower = [], {}, []
        pivot = None
        for j in range(8):
            diagonal = spread(block[j], j)
            pivot = diagonal if j == 0 else jnp.where(sublane == j, diagonal, pivot)
            inverse.append(1.0 / diagonal)
            for q in range(j + 1, 8):
                cross[j, q] = spread(block[j], q)
            if j == 7:
                break
            block[j + 1] = block[j + 1] - (block[j] * cross[j, j + 1]) * inverse[j]
            factor = block[j] * inverse[j]
            lower.append(factor)
            for q in range(j + 2, 8):
                block[q] = block[q] - factor * cross[j, q]
            work = work - jnp.where(sublane > j, factor, 0.0) * spread(work, j)
        scaled = work * lax.rsqrt(pivot)
        top.append(jnp.where((lane < 8 * b + 8) | (lane >= 8 * half), scaled, 0.0))
        done.append(jnp.where(lane < 8 * b + 8, scaled, 0.0))
        if b + 1 == limit:
            continue
        line = [spread(work, j) for j in range(8)]
        for i in range(b + 1, min(b + 3, limit)):
            value, factors = columns(rows[i], b), []
            for j in range(8):
                factors.append(value[j] * inverse[j])
                for q in range(j + 1, 8):
                    value[q] = value[q] - factors[j] * cross[j, q]
            if i == b + 1:
                block = columns(rows[i], i)
                for q in range(8):
                    for j in range(8):
                        block[q] = block[q] - factors[j] * spread(value[j], q)
            new = jnp.where(inside, 0.0, rows[i])
            for j in range(8):
                new = new - factors[j] * line[j]
            rows[i] = new
        if b + 3 >= limit:
            continue
        solved = [None] * 8
        for j in reversed(range(8)):
            value = line[j] * inverse[j]
            for q in range(j + 1, 8):
                value = value - spread(lower[j], q) * solved[q]
            solved[j] = value
        for i in range(b + 3, limit):
            new = jnp.where(inside, 0.0, rows[i])
            entry = columns(rows[i], b)
            for j in range(8):
                new = new - entry[j] * solved[j]
            rows[i] = new
    return done


def basis_kernel(
    high_ref, low_ref, cov_high, cov_low, shift_ref, gram_ref, start_ref, masked_ref,
    loadings_hbm, scores_hbm, explained_ref, loadings_ref, scores_ref, basis_ref, inverse_ref, lsem, ssem,
):
    var = lax.axis_index("var")
    local_vars = masked_ref.shape[0]
    width = local_vars * M
    k = start_ref.shape[1]
    basis_ref[...] = start_ref[...].T

    def sweep(_, carry):
        high, low = split(basis_ref[...])
        both = dot(jnp.concatenate([high, low], axis=0), cov_high[...], NN)
        image = both[0:k] + (both[k:2 * k] + dot(high, cov_low[...], NN))
        gram = dot(image, image, NT, HIGHEST)
        for i, tile in enumerate(inverse_factor(gram)):
            inverse_ref[8 * i:8 * i + 8, :] = tile
        basis_ref[...] = dot(inverse_ref[...], image, NN, HIGHEST)
        return carry

    lax.fori_loop(0, SWEEPS, sweep, 0)

    own = pl.ds(pl.multiple_of(var * width, width), width)
    mine = basis_ref[:, own].astype(BF16)
    flush = []
    for v in range(local_vars):
        loadings_ref[v] = dot(mine[:, v * M:(v + 1) * M], masked_ref[v], NN).astype(BF16)
        flush.append(pltpu.make_async_copy(loadings_ref.at[v], loadings_hbm.at[v], lsem.at[v]))
        flush[v].start()

    high, low = split(basis_ref[...])
    offset = shift_ref[0:1, :]
    tall = jnp.where(lax.broadcasted_iota(jnp.int32, (8, offset.shape[1]), 0) == 0, offset, 0.0)
    both = dot(high_ref[...], jnp.concatenate([high, low], axis=0), NT)
    mean = dot(tall, basis_ref[...], NT, HIGHEST)[0:1, :]
    scores = both[:, 0:k] + (both[:, k:2 * k] + dot(low_ref[...], high, NT)) - mean
    scores_ref[...] = scores
    flush.append(pltpu.make_async_copy(scores_ref, scores_hbm, ssem))
    flush[-1].start()

    scores_low = scores.astype(BF16)
    wide = mine.astype(F32)
    owner = lax.broadcasted_iota(jnp.int32, (k, width), 1) // M
    spread, quads = [], []
    for v in range(local_vars):
        line = wide[:, v * M:(v + 1) * M]
        spread.append(jnp.where(owner == v, 2.0 * wide, 0.0))
        inner = dot(line, gram_ref[:, v * M:(v + 1) * M], NN, HIGHEST)
        quads.append(dot(inner, line, NT, HIGHEST))
    cross = jnp.concatenate(spread, axis=0)
    square = split(-jnp.concatenate(quads, axis=0))
    right = jnp.concatenate([cross.astype(BF16), cross.astype(BF16), square[0], square[1]], axis=1)
    left = jnp.concatenate([high_ref[:, own], low_ref[:, own], scores_low, scores_low], axis=1)
    tall = jnp.where(lax.broadcasted_iota(jnp.int32, (8, width), 0) == 0, shift_ref[0:1, own], 0.0)
    inside = dot(left, right, NT) - dot(tall, cross, NT, HIGHEST)[0:1, :]
    ones = jnp.ones((16, k), BF16)
    scores_wide = scores_low.astype(F32)
    for v in range(local_vars):
        gain = split(scores_wide * inside[:, v * k:(v + 1) * k])
        summed = (dot(ones, gain[0], NT) + dot(ones, gain[1], NT)) / M
        explained_ref[v:v + 1, :] = summed[0:1, :]
    for copy in flush:
        copy.wait()


def finish(high, low, cov_high, cov_low, shift, gram, start, masked):
    local_vars, _, points = masked.shape
    samples, joint = high.shape
    k = start.shape[1]
    return pl.pallas_call(
        basis_kernel,
        out_shape=(
            jax.ShapeDtypeStruct((local_vars, k, points), BF16),
            jax.ShapeDtypeStruct((samples, k), F32),
            jax.ShapeDtypeStruct((local_vars, samples), F32),
        ),
        in_specs=[pl.BlockSpec(memory_space=pltpu.VMEM)] * 8,
        out_specs=(
            pl.BlockSpec(memory_space=pltpu.HBM),
            pl.BlockSpec(memory_space=pltpu.HBM),
            pl.BlockSpec(memory_space=pltpu.VMEM),
        ),
        scratch_shapes=[
            pltpu.VMEM((local_vars, k, points), BF16),
            pltpu.VMEM((samples, k), F32),
            pltpu.VMEM((k, joint), F32),
            pltpu.VMEM((k, k), F32),
            pltpu.SemaphoreType.DMA((local_vars,)),
            pltpu.SemaphoreType.DMA(()),
        ],
        compiler_params=pltpu.CompilerParams(vmem_limit_bytes=48 * 1024 * 1024),
        name="finish",
    )(high, low, cov_high, cov_low, shift, gram, start, masked)


def shards(n, nv, fields, eigenfunctions, start, grid_count):
    high, low, cov_high, cov_low, shift, gram, masked = gather_scores(n, nv, grid_count, fields, eigenfunctions)
    return finish(high, low, cov_high, cov_low, shift, gram, start, masked)


def solution(mesh):
    return jax.shard_map(
        functools.partial(shards, mesh.shape["space"], mesh.shape["var"]),
        mesh=mesh,
        in_specs=(P("var", None, "space"), P("var", None, "space"), P(), P()),
        out_specs=(P("var", None, "space"), P(), P("var", None)),
        check_vma=False,
    )
```
